512 devices in a mesh: brick: 128 (over y, z, core), orb: 4 (over x).
Axes of the slice: x: 4, y: 4, z: 16, core: 2. Of those that a mesh axis runs over, the one named last changes fastest.
Arguments:
- spline_table: float32 [65536, 2048], P('brick', 'orb'), may hold values from -6 to 6
- slot_cell: int32 [128, 256], P('brick'), may hold values from 0 to 124
- slot_offset: int32 [3, 128, 256], P(None, 'brick'), may hold values from 0 to 1023
- inverse: float32 [2048, 65536], P('orb', 'brick'), may hold values from -6 to 6
- old_rows: float32 [16384, 2048], P('brick', 'orb'), may hold values from -12 to 12
- mover_source: int32 [16384], P('brick'), may hold values from 0 to 255, as said below
- mover_column: int32 [16384], P('brick'), may hold values from 0 to 511, as said below
Outputs:
- new_inverse: float32 [2048, 65536], P('orb', 'brick')
- ratios: float32 [10, 16384], P(None, 'brick')
The draws below stay inside these ranges and needn't reach their ends.
Inputs may be any that keep to these rules, and one draw needn't show every extreme that they name: `mover_source`: at most 2 movers of one device come from one brick, and in every draw some brick serves exactly 2 movers of every device. `mover_column`: the 128 entries of one device are distinct.
All inputs are finite; a program needn't handle non-finite values.
Results may differ from the reference program's by a relative error of at most 0.0003.
Values sent between devices are 32-bit elements; how exact they have to be, the bound alone decides.
No kernel may reach another device: no remote copies, remote signals or barrier semaphores. Data moves between devices by JAX's collectives and lax.ppermute only.
A program may use at most 128 MiB of HBM per device.

```python
import math
import jax
import jax.numpy as jnp
from jax import lax

ORBITALS = 2048
CB = 5
OFFQ = 1024
GROUP = 4
MOVERS = 128
EL_DEV = 512
DELAY = 512
PAIR = 2
GP = 512
WALKERS = 32
MOVES = 16384
N_BRICK = 128


def draw_mover_source(key, part):
    slot_total = N_BRICK * PAIR
    tier_key, hottest_key, noise_key, order_key = jax.random.split(jax.random.fold_in(key, 11), 4)
    tiers = jax.random.randint(tier_key, (N_BRICK,), 0, 4)
    hottest = jax.random.randint(hottest_key, (), 0, N_BRICK)
    tiers = jnp.where(jnp.arange(N_BRICK) == hottest, 16, tiers)
    slot_tier = jnp.repeat(tiers, PAIR)
    noise = jax.random.randint(noise_key, (N_BRICK, slot_total), 0, 2 ** 20)
    scores = (slot_tier[None, :] * 2 ** 17 + noise) * slot_total + jnp.arange(slot_total)[None, :]
    chosen = lax.top_k(scores, MOVERS)[1]
    order_keys = jax.random.split(order_key, N_BRICK)
    shuffled = jax.vmap(lambda sub_key, chosen_row: jax.random.permutation(sub_key, chosen_row))(order_keys, chosen)
    return shuffled.reshape(-1).astype(jnp.int32)


def draw_mover_column(key, part):
    column_keys = jax.random.split(jax.random.fold_in(key, 23), N_BRICK)
    picked = jax.vmap(lambda sub_key: jax.random.permutation(sub_key, EL_DEV)[:MOVERS])(column_keys)
    return picked.reshape(-1).astype(jnp.int32)


def inverse_column(base_key, column):
    column_key = jax.random.fold_in(base_key, column)
    return jnp.clip(jax.random.normal(column_key, (ORBITALS,), jnp.float32), -6.0, 6.0)


def draw_inverse(key, part):
    base_key = jax.random.fold_in(key, 31)
    columns = jnp.arange(WALKERS * ORBITALS, dtype=jnp.int32)
    stacked = jax.vmap(lambda column: inverse_column(base_key, column))(columns)
    return jnp.transpose(stacked).astype(jnp.float32)


def draw_old_rows(key, part):
    base_key = jax.random.fold_in(key, 31)
    columns = draw_mover_column(key, part)
    movers = jnp.arange(MOVES, dtype=jnp.int32)
    walker = movers // DELAY
    within = movers % DELAY
    global_column = walker * ORBITALS + within // MOVERS * EL_DEV + columns
    picked = jax.vmap(lambda column: inverse_column(base_key, column))(global_column)
    scale_key = jax.random.fold_in(key, 47)
    factor = jnp.exp(jax.random.uniform(scale_key, (MOVES,), jnp.float32, math.log(0.5), math.log(2.0)))
    return (-factor[:, None] * picked).astype(jnp.float32)


def touch_ends(array, own_key, least, top_value):
    dims = array.shape
    spot = [jax.random.randint(jax.random.fold_in(own_key, axis), (), 0, dims[axis]) for axis in range(len(dims))]
    array = array.at[tuple(spot)].set(least)
    longest = dims.index(max(dims))
    spot[longest] = (spot[longest] + 1) % dims[longest]
    return array.at[tuple(spot)].set(top_value)


def level_of(stream_key, shape, pieces, least, top_value):
    factor_of = 1.0
    for position, parts in pieces:
        steps = jax.random.uniform(jax.random.fold_in(jax.random.fold_in(stream_key, 6), position), (parts,), jnp.float32, least / len(pieces), top_value / len(pieces))
        factor_of = factor_of * jnp.repeat(jnp.exp(steps), shape[position] // parts).reshape((-1,) + (1,) * (len(shape) - 1 - position))
    return factor_of


def normal_values(rng, shape, spread, bound, cuts=(), kind=jnp.bfloat16):
    array = jax.random.normal(rng, shape, jnp.float32) * spread
    if len(cuts) > 0:
        array = level_of(rng, shape, cuts, -0.22, 0.18) * array
    return jnp.clip(array, min=-bound, max=bound).astype(kind)


def setup_inputs(seed: int = 0) -> dict:
    keys = jax.random.split(jax.random.key(seed), 8)
    spline_table = normal_values(keys[0], (N_BRICK * GP, ORBITALS), 1.0, 6.0, ((0, 128), (1, 4)), jnp.float32)
    slot_cell = touch_ends(jax.random.randint(keys[1], (N_BRICK, N_BRICK * PAIR), 0, CB ** 3), jax.random.fold_in(keys[1], 1), 0, (CB ** 3) - 1).astype(jnp.int32)
    slot_offset = touch_ends(jax.random.randint(keys[2], (3, N_BRICK, N_BRICK * PAIR), 0, OFFQ), jax.random.fold_in(keys[2], 1), 0, OFFQ - 1).astype(jnp.int32)
    inverse = draw_inverse(jax.random.fold_in(keys[7], 71), 0)
    old_rows = draw_old_rows(jax.random.fold_in(keys[7], 71), 0)
    mover_source = draw_mover_source(jax.random.fold_in(keys[7], 71), 0)
    mover_column = draw_mover_column(jax.random.fold_in(keys[7], 71), 0)
    return {"spline_table": spline_table, "slot_cell": slot_cell, "slot_offset": slot_offset, "inverse": inverse, "old_rows": old_rows, "mover_source": mover_source, "mover_column": mover_column}


PRECISE = lax.Precision.HIGHEST
DERIVATIVE_ORDERS = ((0, 0, 0), (1, 0, 0), (0, 1, 0), (0, 0, 1), (2, 0, 0), (0, 2, 0), (0, 0, 2), (1, 1, 0), (1, 0, 1), (0, 1, 1))

def spline_basis(param):
    rest = 1.0 - param
    square = param * param
    cubed = square * param
    level_terms = jnp.stack([rest * rest * rest / 6.0, (3.0 * cubed - 6.0 * square + 4.0) / 6.0, (-3.0 * cubed + 3.0 * square + 3.0 * param + 1.0) / 6.0, cubed / 6.0])
    slope_terms = jnp.stack([-0.5 * rest * rest, 1.5 * square - 2.0 * param, -1.5 * square + param + 0.5, 0.5 * square])
    curve_terms = jnp.stack([rest, 3.0 * param - 2.0, 1.0 - 3.0 * param, param])
    return (level_terms, slope_terms, curve_terms)

def axis_weights(cell_pos, param, points):
    offset_grid = jnp.arange(points, dtype=jnp.int32)[None, :] - cell_pos[:, None]
    weight_list = []
    for basis_terms in spline_basis(param):
        weight_row = jnp.zeros(offset_grid.shape, param.dtype)
        for corner in range(4):
            weight_row = weight_row + jnp.where(offset_grid == corner, basis_terms[corner][:, None], 0.0)
        weight_list.append(weight_row)
    return weight_list

def spline_weights(cell_index, offsets):
    grid_side = CB + 3
    cell_x = cell_index // (CB * CB)
    cell_y = cell_index // CB % CB
    cell_z = cell_index % CB
    params = (offsets.astype(jnp.float32) + 0.5) / OFFQ
    along_x = axis_weights(cell_x, params[0], grid_side)
    along_y = axis_weights(cell_y, params[1], grid_side)
    along_z = axis_weights(cell_z, params[2], grid_side)
    stacked_rows = []
    for order_x, order_y, order_z in DERIVATIVE_ORDERS:
        product_xyz = along_x[order_x][:, :, None, None] * along_y[order_y][:, None, :, None] * along_z[order_z][:, None, None, :]
        stacked_rows.append(product_xyz.reshape(product_xyz.shape[0], grid_side ** 3))
    return jnp.stack(stacked_rows)

def mover_rows(mover, spline_table, slot_cell, slot_offset, mover_source):
    source = mover_source[mover]
    brick_id = source // PAIR
    slot_id = mover // MOVERS * PAIR + source % PAIR
    weights = spline_weights(slot_cell[brick_id, slot_id][None], slot_offset[:, brick_id, slot_id][:, None])[:, 0, :]
    brick_table = lax.dynamic_slice_in_dim(spline_table, brick_id * GP, GP, 0)
    return jnp.dot(weights, brick_table, precision=PRECISE)

def reference(spline_table, slot_cell, slot_offset, inverse, old_rows, mover_source, mover_column):
    walker_count = N_BRICK // GROUP

    def one_walker(walker):
        first = walker * DELAY
        movers = first + jnp.arange(DELAY, dtype=jnp.int32)
        new_rows = lax.map(lambda mover: mover_rows(mover, spline_table, slot_cell, slot_offset, mover_source), movers)
        walker_block = lax.dynamic_slice_in_dim(inverse, walker * ORBITALS, ORBITALS, 1)
        columns = jnp.arange(DELAY, dtype=jnp.int32) // MOVERS * EL_DEV + lax.dynamic_slice_in_dim(mover_column, first, DELAY, 0)
        picked = jnp.take(walker_block, columns, axis=1)
        walker_ratios = jnp.einsum('arj,ja->ra', new_rows, picked, precision=PRECISE) / math.sqrt(ORBITALS)
        change = new_rows[:, 0, :] - lax.dynamic_slice_in_dim(old_rows, first, DELAY, 0)
        product_z = jnp.dot(change, walker_block, precision=PRECISE) / ORBITALS
        core_matrix = jnp.eye(DELAY, dtype=product_z.dtype) + jnp.take(product_z, columns, axis=1)
        solved = jnp.linalg.solve(core_matrix, product_z)
        return (walker_block - jnp.dot(picked, solved, precision=PRECISE), walker_ratios)
    blocks, ratio_blocks = lax.map(one_walker, jnp.arange(walker_count, dtype=jnp.int32))
    new_inverse = jnp.transpose(blocks, (1, 0, 2)).reshape(ORBITALS, walker_count * ORBITALS)
    ratios = jnp.transpose(ratio_blocks, (1, 0, 2)).reshape(10, walker_count * DELAY)
    return (new_inverse, ratios)
```

```python
import math

import jax
import jax.numpy as jnp
from jax import lax
from jax.experimental import pallas as pl
from jax.experimental.pallas import tpu as pltpu
from jax.sharding import Mesh
from jax.sharding import PartitionSpec as P

ORBITALS = 2048
CB = 5
OFFQ = 1024
GROUP = 4
MOVERS = 128
SLOTS = 256
WIDTH = 512
GRID_SIDE = CB + 3
DELAY = 512
ORB = 4
CHUNK = MOVERS // ORB
LANES = 128
PARTS = WIDTH // LANES

F32 = jnp.float32
BF16 = jnp.bfloat16
DERIVATIVE_ORDERS = (
    (0, 0, 0),
    (1, 0, 0),
    (0, 1, 0),
    (0, 0, 1),
    (2, 0, 0),
    (0, 2, 0),
    (0, 0, 2),
    (1, 1, 0),
    (1, 0, 1),
    (0, 1, 1),
)
NN = (((1,), (0,)), ((), ()))
NT = (((1,), (1,)), ((), ()))
TN = (((0,), (0,)), ((), ()))

PARAMS = pltpu.CompilerParams(vmem_limit_bytes=48 * 1024 * 1024)


def call(body, out_shapes, scratch=(), scalars=0, loose=0, passes=4):
    def run(*operands):
        held = len(operands) - scalars - loose
        spaces = [pltpu.SMEM] * scalars + [pltpu.VMEM] * held + [pl.ANY] * loose
        return pl.pallas_call(
            body,
            in_specs=[pl.BlockSpec(memory_space=space) for space in spaces],
            out_specs=[pl.BlockSpec(memory_space=pltpu.VMEM) for _ in out_shapes],
            out_shape=[jax.ShapeDtypeStruct(shape, F32) for shape in out_shapes],
            scratch_shapes=list(scratch),
            compiler_params=PARAMS,
            cost_estimate=pl.CostEstimate(
                flops=passes * 2 * DELAY**3, transcendentals=0, bytes_accessed=4 * DELAY**2
            ),
        )(*operands)

    return run


def halves(value):
    high = value.astype(BF16)
    return high, (value - high.astype(F32)).astype(BF16)


def mm(left, right, dims):
    return lax.dot_general(left, right, dims, preferred_element_type=F32)


def mm3(left, right, dims):
    left_high, left_low = halves(left)
    right_high, right_low = halves(right)
    return (
        mm(left_high, right_low, dims) + mm(left_low, right_high, dims)
    ) + mm(left_high, right_high, dims)


def select_rows(choice, right, dims):
    high, low = halves(right)
    return mm(choice, high, dims) + mm(choice, low, dims)


def axis_weights(cell, param):
    rest = 1.0 - param
    square = param * param
    cubed = square * param
    level = (
        rest * rest * rest / 6.0,
        (3.0 * cubed - 6.0 * square + 4.0) / 6.0,
        (-3.0 * cubed + 3.0 * square + 3.0 * param + 1.0) / 6.0,
        cubed / 6.0,
    )
    slope = (
        -0.5 * rest * rest,
        1.5 * square - 2.0 * param,
        -1.5 * square + param + 0.5,
        0.5 * square,
    )
    curve = (rest, 3.0 * param - 2.0, 1.0 - 3.0 * param, param)
    corner_of = lax.broadcasted_iota(jnp.int32, cell.shape, 0).astype(F32) - cell
    out = []
    for terms in (level, slope, curve):
        row = jnp.zeros(cell.shape, F32)
        for corner in range(4):
            row = row + jnp.where(corner_of == float(corner), terms[corner], 0.0)
        out.append(row)
    return out


def slot_values(cell_ref, offset_ref):
    shape = (GRID_SIDE, SLOTS)
    cell = jnp.broadcast_to(cell_ref[...].astype(F32), shape)
    cell_x = jnp.floor((cell + 0.5) * (1.0 / (CB * CB)))
    rest = cell - cell_x * (CB * CB)
    cell_y = jnp.floor((rest + 0.5) * (1.0 / CB))
    cell_z = rest - cell_y * CB
    params = [
        (jnp.broadcast_to(offset_ref[axis].astype(F32), shape) + 0.5) * (1.0 / OFFQ)
        for axis in range(3)
    ]
    return [cell_x, cell_y, cell_z], params


def slot_rows(cell_ref, offset_ref, table_ref):
    cells, params = slot_values(cell_ref, offset_ref)
    along_x, along_y, along_z = [axis_weights(c, t)[0] for c, t in zip(cells, params)]
    pieces = []
    for gx in range(GRID_SIDE):
        for gy in range(GRID_SIDE):
            pieces.append((along_x[gx : gx + 1] * along_y[gy : gy + 1]) * along_z)
    return mm3(jnp.concatenate(pieces, axis=0), table_ref[...], TN)


def as_column(row):
    shape = (MOVERS, MOVERS)
    diagonal = lax.broadcasted_iota(jnp.int32, shape, 0) == lax.broadcasted_iota(
        jnp.int32, shape, 1
    )
    return jnp.sum(jnp.where(diagonal, jnp.broadcast_to(row, shape), 0.0), axis=1, keepdims=True)


def lane_of(source):
    shape = (MOVERS, MOVERS)
    earlier = lax.broadcasted_iota(jnp.int32, shape, 0) < lax.broadcasted_iota(jnp.int32, shape, 1)
    same = jnp.broadcast_to(as_column(source), shape) == jnp.broadcast_to(source, shape)
    taken = jnp.sum(jnp.where(earlier & same, 1.0, 0.0), axis=0, keepdims=True)
    pair = source - 2.0 * jnp.floor((source + 0.5) * 0.5)
    swapped = taken > 0.5
    return jnp.where(swapped, source + 1.0 - 2.0 * pair, source), jnp.where(swapped, 1.0, 0.0)


def hot(match):
    return jnp.where(match, 1.0, 0.0).astype(BF16)


def send_body(
    cell_ref, offset_ref, source_ref, column_ref, table_ref, inverse_ref, own_ref, out_ref
):
    source = source_ref[...].astype(F32)
    column = as_column(column_ref[...].astype(F32))
    position = lax.broadcasted_iota(jnp.int32, (MOVERS, WIDTH), 1).astype(F32)
    own = select_rows(hot(position == column), inverse_ref[...], NT)
    own_ref[...] = own
    lane, _ = lane_of(source)
    slot = lax.broadcasted_iota(jnp.int32, (SLOTS, MOVERS), 0).astype(F32)
    sent = select_rows(hot(slot == lane), own, NN)
    rows = slot_rows(cell_ref, offset_ref, table_ref)
    for part in range(PARTS):
        span = slice(part * LANES, (part + 1) * LANES)
        out_ref[pl.ds(part, SLOTS, stride=2 * PARTS), :] = rows[:, span]
        out_ref[pl.ds(PARTS + part, SLOTS, stride=2 * PARTS), :] = sent[:, span]


def gather_body(place_ref, own_ref, far_ref, pair_ref, out_ref):
    group = place_ref[0]
    out_ref[group] = own_ref[...]
    out_ref[group ^ 2] = far_ref[...]
    out_ref[group ^ 1] = pair_ref[0]
    out_ref[group ^ 3] = pair_ref[1]


def change_body(source_ref, arrived_ref, old_ref, columns_ref, *refs):
    out_ref = refs[-1]
    source = as_column(source_ref[...].astype(F32))
    position = lax.broadcasted_iota(jnp.int32, (MOVERS, SLOTS), 1).astype(F32)
    choice = hot(position == source)
    rows = jnp.concatenate(
        [
            select_rows(choice, arrived_ref[pl.ds(part, SLOTS, stride=2 * PARTS), :], NN)
            for part in range(PARTS)
        ],
        axis=1,
    )
    change = rows - old_ref[...]
    core = mm3(change, columns_ref[...], NT) * (1.0 / ORBITALS)
    for member in range(ORB):
        span = slice(member * CHUNK, (member + 1) * CHUNK)
        out_ref[member, 0:CHUNK] = change[span]
        out_ref[member, CHUNK : 2 * CHUNK] = core[span]


def middle_body(parts_ref, core_ref, change_ref):
    core = [parts_ref[member, CHUNK : 2 * CHUNK] for member in range(ORB)]
    total = (core[0] + core[1]) + (core[2] + core[3])
    for member in range(GROUP * ORB):
        core_ref[member] = total
    for member in range(ORB):
        change_ref[member] = parts_ref[member, 0:CHUNK]


def product_body(place_ref, own_ref, far_ref, pair_ref, here_ref, *refs):
    other_refs, out_ref, rows_ref = refs[:-2], refs[-2], refs[-1]
    group = place_ref[0]
    orb = place_ref[1]
    for member in range(ORB):
        for block, part in (
            (group, own_ref[member]),
            (group ^ 2, far_ref[member]),
            (group ^ 1, pair_ref[0, member]),
            (group ^ 3, pair_ref[1, member]),
        ):
            rows_ref[member, pl.ds(pl.multiple_of(block * CHUNK, CHUNK), CHUNK), :] = part
    total = mm3(rows_ref[orb], here_ref[...], NN)
    for step, other_ref in enumerate(other_refs):
        total += mm3(rows_ref[orb ^ (step + 1)], other_ref[...], NN)
    out_ref[...] = total * (1.0 / ORBITALS)


def total_of(parts_ref):
    return (parts_ref[0] + parts_ref[1]) + (parts_ref[2] + parts_ref[3])


BF16_STEPS = 24
SPLIT_STEPS = 8
FULL_STEPS = 64
COARSE = 0.01
FINE = 1e-5


def solve_body(core_ref, columns_ref, *refs):
    out_ref, full_ref, guess_ref, rest_ref = refs[-4:]
    shape = (DELAY, DELAY)
    identity = jnp.where(
        lax.broadcasted_iota(jnp.int32, shape, 0) == lax.broadcasted_iota(jnp.int32, shape, 1),
        1.0,
        0.0,
    )
    full_ref[...] = core_ref[...] + identity
    size = jnp.abs(full_ref[...])
    bound = jnp.max(jnp.sum(size, axis=0)) * jnp.max(jnp.sum(size, axis=1))

    def start():
        guess_ref[...] = full_ref[...].T * (1.0 / bound)

    def remain(product):
        left = (
            jnp.where(
                lax.broadcasted_iota(jnp.int32, shape, 0)
                == lax.broadcasted_iota(jnp.int32, shape, 1),
                1.0,
                0.0,
            )
            - product
        )
        rest_ref[...] = left
        return jnp.sum(left * left)

    def coarse_step(carry):
        step, _, last = carry
        guess = guess_ref[...].astype(BF16)
        size = remain(mm(full_ref[...].astype(BF16), guess, NN))
        guess_ref[...] += mm(guess, rest_ref[...].astype(BF16), NN)
        return step + 1, last, size

    def coarse_more(carry):
        step, before, last = carry
        stalled = (last < 0.5) & (last > 0.5 * before)
        return (step < BF16_STEPS) & (last > COARSE) & (last < 1e4) & jnp.logical_not(stalled)

    def split_step(carry):
        step, _ = carry
        size = remain(mm3(full_ref[...], guess_ref[...], NN))
        guess_ref[...] += mm(guess_ref[...].astype(BF16), rest_ref[...].astype(BF16), NN)
        return step + 1, size

    def full_step(carry):
        step, _ = carry
        size = remain(
            lax.dot_general(
                full_ref[...],
                guess_ref[...],
                NN,
                precision=lax.Precision.HIGHEST,
                preferred_element_type=F32,
            )
        )
        guess_ref[...] += lax.dot_general(
            guess_ref[...],
            rest_ref[...],
            NN,
            precision=lax.Precision.HIGHEST,
            preferred_element_type=F32,
        )
        return step + 1, size

    start()
    _, _, coarse = lax.while_loop(coarse_more, coarse_step, (0, F32(1e3), F32(1e3)))
    usable = coarse < 0.5
    _, split = lax.while_loop(
        lambda c: (c[0] < SPLIT_STEPS) & (c[1] > FINE) & (c[1] < 1e4),
        split_step,
        (jnp.where(usable, 0, SPLIT_STEPS), F32(1e3)),
    )
    settled = split <= FINE

    @pl.when(jnp.logical_not(settled))
    def _():
        start()

    lax.while_loop(
        lambda c: (c[0] < FULL_STEPS) & (c[1] > 1e-9),
        full_step,
        (jnp.where(settled, FULL_STEPS, 0), F32(1e3)),
    )
    out_ref[...] = mm3(columns_ref[...], guess_ref[...], TN)


def finish_body(place_ref, inverse_ref, left_ref, own_ref, *refs):
    other_refs, out_ref, product_ref = refs[:-2], refs[-2], refs[-1]
    orb = place_ref[1]
    for step, part_ref in enumerate((own_ref, *other_refs)):
        first = (orb ^ step) * CHUNK
        for group in range(GROUP):
            row = pl.multiple_of(group * MOVERS + first, CHUNK)
            product_ref[pl.ds(row, CHUNK), :] = part_ref[group * CHUNK : (group + 1) * CHUNK]
    out_ref[...] = inverse_ref[...] - mm3(left_ref[...], product_ref[...], NN)


def ratio_values(grid_ref, cells, params):
    along = [axis_weights(c, t) for c, t in zip(cells, params)]
    side = GRID_SIDE
    by_x = {}
    for order in range(3):
        planes = []
        for gy in range(side):
            total = None
            for gx in range(side):
                first = (gx * side + gy) * side
                term = along[0][order][gx : gx + 1] * grid_ref[first : first + side, :]
                total = term if total is None else total + term
            planes.append(total)
        by_x[order] = planes
    by_xy = {}
    for order_x, order_y in ((0, 0), (1, 0), (0, 1), (2, 0), (0, 2), (1, 1)):
        total = None
        for gy in range(side):
            term = along[1][order_y][gy : gy + 1] * by_x[order_x][gy]
            total = term if total is None else total + term
        by_xy[order_x, order_y] = total
    return [
        jnp.sum(along[2][oz] * by_xy[ox, oy], axis=0, keepdims=True)
        for ox, oy, oz in DERIVATIVE_ORDERS
    ]


def ratio_body(cell_ref, offset_ref, table_ref, arrived_ref, *refs):
    out_ref, grid_ref, turn_ref = refs[-3:]
    columns = jnp.concatenate(
        [
            arrived_ref[pl.ds(PARTS + part, SLOTS, stride=2 * PARTS), :]
            for part in range(PARTS)
        ],
        axis=1,
    )
    grid_ref[...] = mm3(table_ref[...], columns, NT)
    cells, params = slot_values(cell_ref, offset_ref)
    odd = lax.broadcasted_iota(jnp.int32, (GRID_SIDE, SLOTS), 1) % 2 == 1

    def other(value):
        return jnp.where(odd, pltpu.roll(value, 1, 1), pltpu.roll(value, SLOTS - 1, 1))

    values = ratio_values(grid_ref, cells, params)
    values += ratio_values(grid_ref, [other(c) for c in cells], [other(t) for t in params])
    values.append(jnp.zeros((LANES - len(values), SLOTS), F32))
    turn_ref[...] = jnp.concatenate(values, axis=0).T
    half = SLOTS // 2
    out_ref[...] = turn_ref[pl.ds(0, half, stride=2), :] + pltpu.roll(
        turn_ref[pl.ds(1, half, stride=2), :], LANES // 2, 1
    )


COUNT = len(DERIVATIVE_ORDERS)


def ratio_pick_body(source_ref, values_ref, out_ref):
    lane, swapped = lane_of(source_ref[...].astype(F32))
    brick = jnp.floor((lane + 0.5) * 0.5)
    pair = lane - 2.0 * brick
    position = lax.broadcasted_iota(jnp.int32, (MOVERS, MOVERS), 0).astype(F32)
    choice = hot(position == brick)
    value = values_ref[...]
    high = value.astype(BF16)
    rest = value - high.astype(F32)
    middle = rest.astype(BF16)
    low = (rest - middle.astype(F32)).astype(BF16)
    picked = (mm(low, choice, TN) + mm(middle, choice, TN)) + mm(high, choice, TN)
    half = LANES // 2

    both = []
    for first in (0, half):
        both.append((picked[first : first + COUNT], picked[first + COUNT : first + 2 * COUNT]))
    chosen = []
    for straight, crossed in both:
        chosen.append(jnp.where(swapped > 0.5, crossed, straight))
    value = jnp.where(pair > 0.5, chosen[1], chosen[0])
    out = jnp.concatenate([value, jnp.zeros((16 - COUNT, MOVERS), F32)], axis=0)
    for member in range(ORB):
        out_ref[member] = out


def ratio_sum_body(parts_ref, out_ref):
    out_ref[...] = total_of(parts_ref)[:COUNT] * (1.0 / math.sqrt(ORBITALS))


def exchange(value, axes):
    return lax.all_to_all(value, axes, 0, 0, tiled=True)


def swap(value, axis, mask):
    return lax.ppermute(value, axis, [(device, device ^ mask) for device in range(4)])


def local(spline_table, slot_cell, slot_offset, inverse, old_rows, mover_source, mover_column):
    source = mover_source.reshape(1, MOVERS)
    column = mover_column.reshape(1, MOVERS)
    brick = ("walker", "group")
    tiles = SLOTS * 2 * PARTS
    place = jnp.stack([lax.axis_index("group"), lax.axis_index("orb")]).astype(jnp.int32)

    own_columns, sent = call(send_body, [(MOVERS, WIDTH), (tiles, LANES)])(
        slot_cell, slot_offset, source, column, spline_table, inverse
    )
    arrived = exchange(sent.reshape(tiles // 16, 16, LANES), brick).reshape(tiles, LANES)

    far_columns = swap(own_columns, "group", 2)
    pair_columns = swap(jnp.stack([own_columns, far_columns]), "group", 1)
    (columns,) = call(gather_body, [(GROUP, MOVERS, WIDTH)], scalars=1)(
        place, own_columns, far_columns, pair_columns
    )
    columns = columns.reshape(DELAY, WIDTH)
    kept, _ = lax.optimization_barrier((inverse, own_columns))
    inverses = [swap(kept, "orb", mask) for mask in range(1, ORB)]

    (parts,) = call(change_body, [(ORB, 2 * CHUNK, WIDTH)], loose=ORB - 1)(
        source, arrived, old_rows, columns, *inverses
    )
    core_rows, change = call(middle_body, [(GROUP * ORB, CHUNK, DELAY), (ORB, CHUNK, WIDTH)])(
        exchange(parts, "orb")
    )
    core = exchange(core_rows, ("group", "orb")).reshape(DELAY, DELAY)

    far_change = swap(change, "group", 2)
    pair_change = swap(jnp.stack([change, far_change]), "group", 1)
    (product,) = call(
        product_body, [(MOVERS, WIDTH)], [pltpu.VMEM((ORB, MOVERS, WIDTH), F32)], scalars=1
    )(place, change, far_change, pair_change, inverse, *inverses)
    products = [swap(product, "orb", mask) for mask in range(1, ORB)]

    (ratio_part,) = call(
        ratio_body,
        [(SLOTS // 2, LANES)],
        [pltpu.VMEM((GRID_SIDE**3, SLOTS), F32), pltpu.VMEM((SLOTS, LANES), F32)],
        loose=1,
    )(slot_cell, slot_offset, spline_table, arrived, core)
    ratio_back = exchange(ratio_part.reshape(SLOTS // 2, 1, LANES), brick)

    square = pltpu.VMEM((DELAY, DELAY), F32)
    (left,) = call(solve_body, [(WIDTH, DELAY)], [square, square, square], loose=2, passes=64)(
        core, columns, ratio_part, product
    )
    (new_inverse,) = call(
        finish_body, [(WIDTH, WIDTH)], [pltpu.VMEM((DELAY, WIDTH), F32)], scalars=1
    )(place, inverse, left, product, *products)

    (ratio_own,) = call(ratio_pick_body, [(ORB, 16, MOVERS)])(
        source, ratio_back.reshape(SLOTS // 2, LANES)
    )
    (ratios,) = call(ratio_sum_body, [(COUNT, MOVERS)])(exchange(ratio_own, "orb"))
    return new_inverse, ratios


def solution(mesh):
    devices = mesh.devices
    inner = Mesh(
        devices.reshape(devices.shape[0] // GROUP, GROUP, devices.shape[1]),
        ("walker", "group", "orb"),
    )
    brick = ("walker", "group")
    in_specs = (
        P(brick, "orb"),
        P(brick, None),
        P(None, brick, None),
        P("orb", brick),
        P(brick, "orb"),
        P(brick),
        P(brick),
    )
    out_specs = (P("orb", brick), P(None, brick))
    return jax.shard_map(local, mesh=inner, in_specs=in_specs, out_specs=out_specs, check_vma=False)
```
